32 devices in a mesh: occ: 16 (over z, x, core), vir: 2 (over y).
Axes of the slice: x: 2, y: 2, z: 4, core: 2. Of those that a mesh axis runs over, the one named last changes fastest.
Arguments:
- factors: bfloat16 [16, 1024, 3072], P('occ', 'vir'), may hold values from -0.71875 to 0.71875
- occ_energy: float32 [16], replicated, may hold values from -2 to -0.4
- vir_energy: float32 [1024], replicated, may hold values from 0.4 to 4
- density_in: float32 [16, 1024, 3072], P('occ', 'vir'), may hold values from -3 to 3
Outputs:
- density: float32 [16, 1024, 3072], P('occ', 'vir')
The draws below stay inside these ranges and needn't reach their ends.
All inputs are finite; a program needn't handle non-finite values.
Results may differ from the reference program's by a relative error of at most 0.0027.
Values may be sent and summed in bfloat16 or wider, within the bound.
A program may use at most 128 MiB of HBM per device.

```python
import jax
import jax.numpy as jnp
from jax import lax

V = 1024
X = 3072
OCC_DEV = 1
VISITS = 3
OCC = 16
N_OCC = 16


def block_scale(key, extent, cuts, low, largest):
    gain, own = 1.0, jax.random.fold_in(key, 6)
    for axis_at, parts in cuts:
        steps = jnp.exp(jax.random.uniform(jax.random.fold_in(own, axis_at), (parts,), jnp.float32, low / len(cuts), largest / len(cuts)))
        gain = gain * jnp.repeat(steps, extent[axis_at] // parts).reshape([-1 if axis == axis_at else 1 for axis in range(len(extent))])
    return gain


def gaussian(stream_key, shape, deviation, most, shards=(), held_as=jnp.bfloat16):
    drawn = deviation * jax.random.normal(stream_key, shape, jnp.float32)
    if shards:
        drawn = drawn * block_scale(stream_key, shape, shards, -0.22, 0.18)
    return jnp.clip(drawn, -most, most).astype(held_as)


def setup_inputs(seed: int = 0) -> dict:
    arg_keys = jax.random.split(jax.random.key(seed), 5)
    return {
        "factors": gaussian(arg_keys[0], (OCC, V, X), 0.12, 0.71875, ((0, 16), (1, 2))),
        "occ_energy": jnp.clip(jax.random.uniform(arg_keys[1], (OCC,), jnp.float32, -2.0, -0.4), -2.0, -0.4),
        "vir_energy": jnp.clip(jax.random.uniform(arg_keys[2], (V,), jnp.float32, 0.4, 4.0), 0.4, 4.0),
        "density_in": gaussian(arg_keys[3], (OCC, V, X), 0.5, 3.0, ((0, 16), (1, 2)), jnp.float32),
    }


def to_half(value):
    return lax.optimization_barrier(value.astype(jnp.bfloat16)).astype(jnp.float32)


def reference(factors, occ_energy, vir_energy, density_in):
    widened = factors.astype(jnp.float32)

    def one_block(block):
        start = (block * OCC_DEV).astype(jnp.int32)
        own = lax.dynamic_slice_in_dim(widened, start, OCC_DEV, 0)
        e_own = lax.dynamic_slice_in_dim(occ_energy, start, OCC_DEV, 0)
        total = jnp.zeros((OCC_DEV * V, X), jnp.float32)
        for visit in range(VISITS):
            other = (((block - visit) % N_OCC) * OCC_DEV).astype(jnp.int32)
            partner = lax.dynamic_slice_in_dim(widened, other, OCC_DEV, 0)
            e_partner = lax.dynamic_slice_in_dim(occ_energy, other, OCC_DEV, 0)
            direct = jnp.dot(own.reshape(OCC_DEV * V, X), partner.reshape(OCC_DEV * V, X).T,
                             precision=lax.Precision.HIGHEST)
            tile = to_half(direct).reshape(OCC_DEV, V, OCC_DEV, V)
            swapped = tile.transpose(0, 3, 2, 1)
            denom = (e_own[:, None, None, None] + e_partner[None, None, :, None]
                     - vir_energy[None, :, None, None] - vir_energy[None, None, None, :])
            amp = to_half((2.0 * tile - swapped) / denom)
            total = total + jnp.dot(amp.reshape(OCC_DEV * V, OCC_DEV * V), partner.reshape(OCC_DEV * V, X),
                                    precision=lax.Precision.HIGHEST)
        return total.reshape(OCC_DEV, V, X)

    blocks = lax.map(one_block, jnp.arange(N_OCC, dtype=jnp.int32))
    return density_in + blocks.reshape(OCC_DEV * N_OCC, V, X)
```

```python
import jax
import jax.numpy as jnp
from jax import lax
from jax.sharding import PartitionSpec as P


def passed_along(block, axis, distance):
    size = lax.axis_size(axis)
    return lax.ppermute(block, axis, [((i - distance) % size, i) for i in range(size)])


def swapped_cores(block):
    return lax.ppermute(block, "occ", [(i ^ 1, i) for i in range(lax.axis_size("occ"))])


def product(left, right):
    return lax.dot_general(
        left, right, (((1,), (1,)), ((), ())), preferred_element_type=jnp.float32
    ).astype(jnp.bfloat16)


def on_device(factors, occ_energy, vir_energy, density_in):
    vir_local, aux_width = factors.shape[1:]
    occ_rank = lax.axis_index("occ")
    cycle_size = lax.axis_size("occ")
    vir_rank = lax.axis_index("vir")
    vir_size = lax.axis_size("vir")
    first_core = occ_rank % 2 == 0
    half = vir_local // 2
    mine = factors.reshape(vir_local, aux_width)
    low, high = mine[:half], mine[half:]
    own = [(low, high)]
    far = [(passed_along(low, "occ", 2), passed_along(high, "occ", 2))]
    for d in range(1, vir_size):
        own.append((passed_along(low, "vir", d), passed_along(high, "vir", d)))
    for d in range(1, vir_size):
        far.append((passed_along(far[0][0], "vir", d), passed_along(own[d][1], "occ", 2)))
    near = []
    for d in range(vir_size):
        near.append(tuple(swapped_cores(jnp.where(first_core, o, f)) for o, f in zip(own[d], far[d])))

    def energies(d):
        rank = (vir_rank - d) % vir_size
        return lax.dynamic_slice_in_dim(vir_energy, rank * vir_local, vir_local, 0)

    e_own = occ_energy[occ_rank]
    own = [jnp.concatenate(pair) if d else mine for d, pair in enumerate(own)]
    far = [jnp.concatenate(pair) for pair in far]
    near = [jnp.concatenate(pair) for pair in near]
    total = density_in.reshape(vir_local, aux_width)
    for d in range(vir_size):
        for visit, partner in ((0, own), (2, far), (1, near)):
            e_partner = occ_energy[(occ_rank - visit) % cycle_size]
            direct = product(mine, partner[d])
            swapped = direct if visit == 0 else product(partner[0], own[d])
            denom = e_own + e_partner - energies(0)[:, None] - energies(d)[None, :]
            amp = (2.0 * direct.astype(jnp.float32) - swapped.astype(jnp.float32)) / denom
            total = total + jnp.dot(
                amp.astype(jnp.bfloat16), partner[d], preferred_element_type=jnp.float32
            )
    return total.reshape(density_in.shape)


def solution(mesh):
    return jax.shard_map(
        on_device,
        mesh=mesh,
        in_specs=(P("occ", "vir", None), P(), P(), P("occ", "vir", None)),
        out_specs=P("occ", "vir", None),
        check_vma=False,
    )
```

```python
import functools

import jax
import jax.numpy as jnp
from jax import lax
from jax.experimental import pallas as pl
from jax.experimental.pallas import tpu as pltpu
from jax.sharding import PartitionSpec as P

MESH = pl.DeviceIdType.MESH
OWN, NEAR, FAR = 0, 1, 2


def product(left, right):
    out = lax.dot_general(
        left, right, (((1,), (1,)), ((), ())), preferred_element_type=jnp.float32
    )
    return out.astype(jnp.bfloat16).astype(jnp.float32)


def kernel(
    n, cycle, e_pair, e_rows, e_cols, factors, density_in, out,
    buf, acc, direct, swapped, send, recv, local,
):
    pairs, _, r, aux = factors.shape
    w = 2 * r
    h = pairs * w
    i, v = lax.axis_index("occ"), lax.axis_index("vir")
    even = lax.rem(i, 2) == 0
    peer = i + 1 - 2 * lax.rem(i, 2)
    ahead, behind = lax.rem(i + 2, cycle), lax.rem(i + cycle - 2, cycle)

    load_own = pltpu.make_async_copy(factors, buf.at[OWN, 0], local.at[0])
    load_acc = pltpu.make_async_copy(density_in, acc, local.at[1])
    load_own.start()
    load_acc.start()

    barrier = pltpu.get_barrier_semaphore()
    for other in (ahead, behind, peer):
        pl.semaphore_signal(barrier, inc=1, device_id={"occ": other}, device_id_type=MESH)
    for d in range(1, n):
        pl.semaphore_signal(barrier, inc=1, device_id={"vir": lax.rem(v + d, n)}, device_id_type=MESH)
    pl.semaphore_wait(barrier, n + 2)

    def move(src, kind, d, p, q, device):
        return pltpu.make_async_remote_copy(
            src_ref=src,
            dst_ref=buf.at[kind, d, p, q],
            send_sem=send.at[kind, d, p, q],
            recv_sem=recv.at[kind, d, p, q],
            device_id=device,
            device_id_type=MESH,
        )

    def arrived(kind, d, p, q):
        move(buf.at[kind, d, p, q], kind, d, p, q, {"occ": peer}).wait_recv()

    def along_vir(d):
        return {"vir": lax.rem(v + d, n)}

    for p in range(pairs):
        for q in range(2):
            for d in range(1, n):
                move(factors.at[p, q], OWN, d, p, q, along_vir(d)).start()
            move(factors.at[p, q], FAR, 0, p, q, {"occ": ahead}).start()

            @pl.when(even)
            def _():
                move(factors.at[p, q], NEAR, 0, p, q, {"occ": peer}).start()

    def block(kind):
        return buf[kind, 0].reshape(h, aux)

    def pair(kind, d, p):
        return buf[kind, d, p].reshape(w, aux)

    tile = 1024 if aux % 1024 == 0 else aux

    def contribute(kind, d, p, m, s):
        denom = e_pair[kind] - e_rows[...] - e_cols[d, p]
        amp = ((2.0 * m - s) / denom).astype(jnp.bfloat16)

        def column(c, _):
            at = pl.ds(pl.multiple_of(c * tile, tile), tile)
            acc[:, at] += jnp.dot(
                amp, buf[kind, d, p, :, :, at].reshape(w, tile), preferred_element_type=jnp.float32
            )
            return 0

        lax.fori_loop(0, aux // tile, column, 0)

    def own_pair(d, p):
        m = product(block(OWN), pair(OWN, d, p))
        contribute(OWN, d, p, m, m)

    load_own.wait()
    load_acc.wait()

    def first(p, _):
        own_pair(0, p)
        return 0

    lax.fori_loop(0, pairs, first, 0)

    def second(p, _):
        for q in range(2):
            arrived(FAR, 0, p, q)

            @pl.when(even == False)
            def _():
                move(buf.at[FAR, 0, p, q], NEAR, 0, p, q, {"occ": peer}).start()

        for d in range(1, n):
            move(buf.at[FAR, 0, p, 0], FAR, d, p, 0, along_vir(d)).start()

        def whole(d, _):
            for q in range(2):
                arrived(OWN, d, p, q)

                @pl.when(even)
                def _():
                    move(buf.at[OWN, d, p, q], NEAR, d, p, q, {"occ": peer}).start()

            move(buf.at[OWN, d, p, 1], FAR, d, p, 1, {"occ": ahead}).start()
            own_pair(d, p)
            return 0

        lax.fori_loop(1, n, whole, 0)
        direct[FAR - 1, p] = product(block(OWN), pair(FAR, 0, p))
        return 0

    lax.fori_loop(0, pairs, second, 0)

    def third(step, _):
        kind = FAR - step

        @pl.when(step == 1)
        def _():
            def near(p, _):
                arrived(NEAR, 0, p, 0)
                arrived(NEAR, 0, p, 1)
                direct[NEAR - 1, p] = product(block(OWN), pair(NEAR, 0, p))
                return 0

            lax.fori_loop(0, pairs, near, 0)

        def diagonal(p, _):
            at = pl.ds(pl.multiple_of(p * w, w), w)
            s = jnp.concatenate([direct[kind - 1, b, at, :].T for b in range(pairs)], axis=0)
            contribute(kind, 0, p, direct[kind - 1, p], s)

            def other(d, _):
                swapped[kind - 1, d, p] = product(block(kind), pair(OWN, d, p))
                return 0

            lax.fori_loop(1, n, other, 0)
            return 0

        lax.fori_loop(0, pairs, diagonal, 0)
        return 0

    lax.fori_loop(0, 2, third, 0)

    def fourth(step, _):
        p, d = step // (n - 1), 1 + lax.rem(step, n - 1)
        for q in range(2):
            arrived(FAR, d, p, q)

            @pl.when(even == False)
            def _():
                move(buf.at[FAR, d, p, q], NEAR, d, p, q, {"occ": peer}).start()

        def finish(turn, _):
            kind = FAR - turn

            @pl.when(turn == 1)
            def _():
                arrived(NEAR, d, p, 0)
                arrived(NEAR, d, p, 1)

            m = product(block(OWN), pair(kind, d, p))
            contribute(kind, d, p, m, swapped[kind - 1, d, p])
            return 0

        lax.fori_loop(0, 2, finish, 0)
        return 0

    lax.fori_loop(0, pairs * (n - 1), fourth, 0)

    store = pltpu.make_async_copy(acc, out, local.at[1])
    store.start()

    for p in range(pairs):
        for q in range(2):
            for kind in (OWN, NEAR, FAR):
                for d in range(1 if kind == OWN else 0, n):
                    move(buf.at[kind, d, p, q], kind, d, p, q, {"occ": peer}).wait_send()
    store.wait()


def on_device(factors, occ_energy, vir_energy, density_in):
    h, aux = factors.shape[1:]
    n, cycle = lax.axis_size("vir"), lax.axis_size("occ")
    i, v = lax.axis_index("occ"), lax.axis_index("vir")
    w = 256 if h % 256 == 0 else h
    pairs = h // w
    e_pair = occ_energy[i] + occ_energy[(i - jnp.arange(3)) % cycle]
    ranks = (v - jnp.arange(n)) % n
    by_rank = vir_energy.reshape(n, h)[ranks]
    vmem = pl.BlockSpec(memory_space=pltpu.VMEM)
    hbm = pl.BlockSpec(memory_space=pl.ANY)
    out = pl.pallas_call(
        functools.partial(kernel, n, cycle),
        out_shape=jax.ShapeDtypeStruct((h, aux), jnp.float32),
        in_specs=[pl.BlockSpec(memory_space=pltpu.SMEM), vmem, vmem, hbm, hbm],
        out_specs=hbm,
        scratch_shapes=[
            pltpu.VMEM((3, n, pairs, 2, w // 2, aux), jnp.bfloat16),
            pltpu.VMEM((h, aux), jnp.float32),
            pltpu.VMEM((2, pairs, h, w), jnp.float32),
            pltpu.VMEM((2, n, pairs, h, w), jnp.float32),
            pltpu.SemaphoreType.DMA((3, n, pairs, 2)),
            pltpu.SemaphoreType.DMA((3, n, pairs, 2)),
            pltpu.SemaphoreType.DMA((2,)),
        ],
        compiler_params=pltpu.CompilerParams(
            collective_id=0, has_side_effects=True, vmem_limit_bytes=60 * 1024 * 1024
        ),
    )(
        e_pair,
        by_rank[0][:, None],
        by_rank.reshape(n, pairs, 1, w),
        factors.reshape(pairs, 2, w // 2, aux),
        density_in.reshape(h, aux),
    )
    return out.reshape(density_in.shape)


def solution(mesh):
    return jax.shard_map(
        on_device,
        mesh=mesh,
        in_specs=(P("occ", "vir", None), P(), P(), P("occ", "vir", None)),
        out_specs=P("occ", "vir", None),
        check_vma=False,
    )
```

```python
import functools

import jax
import jax.numpy as jnp
from jax import lax
from jax.experimental import pallas as pl
from jax.experimental.pallas import tpu as pltpu
from jax.sharding import PartitionSpec as P

MESH = pl.DeviceIdType.MESH
OWN, NEAR, FAR = 0, 1, 2


def product(left, right):
    out = lax.dot_general(
        left, right, (((1,), (1,)), ((), ())), preferred_element_type=jnp.float32
    )
    return out.astype(jnp.bfloat16).astype(jnp.float32)


def kernel(
    n, cycle, e_occ, e_vir, factors, density_in, out,
    buf, acc, direct, swapped, e_rows, send, recv, local,
):
    pairs, _, r, aux = factors.shape
    w = 2 * r
    h = pairs * w
    i, v = lax.axis_index("occ"), lax.axis_index("vir")
    even = lax.rem(i, 2) == 0
    peer = i + 1 - 2 * lax.rem(i, 2)
    ahead, behind = lax.rem(i + 2, cycle), lax.rem(i + cycle - 2, cycle)

    load_own = pltpu.make_async_copy(factors, buf.at[OWN, 0], local.at[0])
    load_acc = pltpu.make_async_copy(density_in, acc, local.at[1])
    load_own.start()
    load_acc.start()

    barrier = pltpu.get_barrier_semaphore()
    for other in (ahead, behind, peer):
        pl.semaphore_signal(barrier, inc=1, device_id={"occ": other}, device_id_type=MESH)
    for d in range(1, n):
        pl.semaphore_signal(barrier, inc=1, device_id={"vir": lax.rem(v + d, n)}, device_id_type=MESH)
    pl.semaphore_wait(barrier, n + 2)

    def move(src, kind, d, p, q, device):
        return pltpu.make_async_remote_copy(
            src_ref=src,
            dst_ref=buf.at[kind, d, p, q],
            send_sem=send.at[kind, d, p, q],
            recv_sem=recv.at[kind, d, p, q],
            device_id=device,
            device_id_type=MESH,
        )

    def arrived(kind, d, p, q):
        move(buf.at[kind, d, p, q], kind, d, p, q, {"occ": peer}).wait_recv()

    def along_vir(d):
        return {"vir": lax.rem(v + d, n)}

    for p in range(pairs):
        for q in range(2):
            for d in range(1, n):
                move(factors.at[p, q], OWN, d, p, q, along_vir(d)).start()
            move(factors.at[p, q], FAR, 0, p, q, {"occ": ahead}).start()

            @pl.when(even)
            def _():
                move(factors.at[p, q], NEAR, 0, p, q, {"occ": peer}).start()

    def block(kind):
        return buf[kind, 0].reshape(h, aux)

    def pair(kind, d, p):
        return buf[kind, d, p].reshape(w, aux)

    tile = 1024 if aux % 1024 == 0 else aux

    def store(c):
        at = pl.ds(pl.multiple_of(c * tile, tile), tile)
        return pltpu.make_async_copy(acc.at[:, at], out.at[:, at], local.at[2 + c])

    def contribute(kind, d, p, m, s, last=None):
        partner = e_occ[lax.rem(i - kind + cycle, cycle)]
        denom = e_occ[i] + partner - e_rows[:, :1] - e_vir[lax.rem(v - d + n, n), p]
        amp = ((2.0 * m - s) / denom).astype(jnp.bfloat16)

        def column(c, _):
            at = pl.ds(pl.multiple_of(c * tile, tile), tile)
            acc[:, at] += jnp.dot(
                amp, buf[kind, d, p, :, :, at].reshape(w, tile), preferred_element_type=jnp.float32
            )
            if last is not None:

                @pl.when(last)
                def _():
                    store(c).start()

            return 0

        lax.fori_loop(0, aux // tile, column, 0)

    def own_pair(d, p):
        m = product(block(OWN), pair(OWN, d, p))
        contribute(OWN, d, p, m, m)

    for p in range(pairs):
        e_rows[p * w : (p + 1) * w, :] = jnp.broadcast_to(e_vir[v, p], (128, w)).T
    load_own.wait()
    load_acc.wait()

    def first(p, _):
        own_pair(0, p)
        return 0

    lax.fori_loop(0, pairs, first, 0)

    def second(p, _):
        for q in range(2):
            arrived(FAR, 0, p, q)

            @pl.when(even == False)
            def _():
                move(buf.at[FAR, 0, p, q], NEAR, 0, p, q, {"occ": peer}).start()

        for d in range(1, n):
            move(buf.at[FAR, 0, p, 0], FAR, d, p, 0, along_vir(d)).start()

        def whole(d, _):
            for q in range(2):
                arrived(OWN, d, p, q)

                @pl.when(even)
                def _():
                    move(buf.at[OWN, d, p, q], NEAR, d, p, q, {"occ": peer}).start()

            move(buf.at[OWN, d, p, 1], FAR, d, p, 1, {"occ": ahead}).start()
            own_pair(d, p)
            return 0

        lax.fori_loop(1, n, whole, 0)
        direct[FAR - 1, p] = product(block(OWN), pair(FAR, 0, p))
        return 0

    lax.fori_loop(0, pairs, second, 0)

    def third(step, _):
        kind = FAR - step

        @pl.when(step == 1)
        def _():
            def near(p, _):
                arrived(NEAR, 0, p, 0)
                arrived(NEAR, 0, p, 1)
                direct[NEAR - 1, p] = product(block(OWN), pair(NEAR, 0, p))
                return 0

            lax.fori_loop(0, pairs, near, 0)

        def diagonal(p, _):
            at = pl.ds(pl.multiple_of(p * w, w), w)
            s = jnp.concatenate([direct[kind - 1, b, at, :].T for b in range(pairs)], axis=0)
            contribute(kind, 0, p, direct[kind - 1, p], s)

            def other(d, _):
                swapped[kind - 1, d, p] = product(block(kind), pair(OWN, d, p))
                return 0

            lax.fori_loop(1, n, other, 0)
            return 0

        lax.fori_loop(0, pairs, diagonal, 0)
        return 0

    lax.fori_loop(0, 2, third, 0)

    def fourth(step, _):
        p, d = step // (n - 1), 1 + lax.rem(step, n - 1)
        for q in range(2):
            arrived(FAR, d, p, q)

            @pl.when(even == False)
            def _():
                move(buf.at[FAR, d, p, q], NEAR, d, p, q, {"occ": peer}).start()

        def finish(turn, _):
            kind = FAR - turn

            @pl.when(turn == 1)
            def _():
                arrived(NEAR, d, p, 0)
                arrived(NEAR, d, p, 1)

            m = product(block(OWN), pair(kind, d, p))
            last = (step == pairs * (n - 1) - 1) & (turn == 1)
            contribute(kind, d, p, m, swapped[kind - 1, d, p], last)
            return 0

        lax.fori_loop(0, 2, finish, 0)
        return 0

    lax.fori_loop(0, pairs * (n - 1), fourth, 0)

    for p in range(pairs):
        for q in range(2):
            for kind in (OWN, NEAR, FAR):
                for d in range(1 if kind == OWN else 0, n):
                    move(buf.at[kind, d, p, q], kind, d, p, q, {"occ": peer}).wait_send()
    for c in range(aux // tile):
        store(c).wait()


def on_device(factors, occ_energy, vir_energy, density_in):
    h, aux = factors.shape[1:]
    n, cycle = lax.axis_size("vir"), lax.axis_size("occ")
    w = 256 if h % 256 == 0 else h
    pairs = h // w
    vmem = pl.BlockSpec(memory_space=pltpu.VMEM)
    hbm = pl.BlockSpec(memory_space=pl.ANY)
    out = pl.pallas_call(
        functools.partial(kernel, n, cycle),
        out_shape=jax.ShapeDtypeStruct((h, aux), jnp.float32),
        in_specs=[pl.BlockSpec(memory_space=pltpu.SMEM), vmem, hbm, hbm],
        out_specs=hbm,
        scratch_shapes=[
            pltpu.VMEM((3, n, pairs, 2, w // 2, aux), jnp.bfloat16),
            pltpu.VMEM((h, aux), jnp.float32),
            pltpu.VMEM((2, pairs, h, w), jnp.float32),
            pltpu.VMEM((2, n, pairs, h, w), jnp.float32),
            pltpu.VMEM((h, 128), jnp.float32),
            pltpu.SemaphoreType.DMA((3, n, pairs, 2)),
            pltpu.SemaphoreType.DMA((3, n, pairs, 2)),
            pltpu.SemaphoreType.DMA((2 + max(1, aux // 1024),)),
        ],
        compiler_params=pltpu.CompilerParams(
            collective_id=0, has_side_effects=True, vmem_limit_bytes=60 * 1024 * 1024
        ),
    )(
        occ_energy,
        vir_energy.reshape(n, pairs, 1, w),
        factors.reshape(pairs, 2, w // 2, aux),
        density_in.reshape(h, aux),
    )
    return out.reshape(density_in.shape)


def solution(mesh):
    return jax.shard_map(
        on_device,
        mesh=mesh,
        in_specs=(P("occ", "vir", None), P(), P(), P("occ", "vir", None)),
        out_specs=P("occ", "vir", None),
        check_vma=False,
    )
```
